32 devices in a mesh: segment: 4 (over x, core), rows: 8 (over z, y).
Axes of the slice: x: 2, y: 2, z: 4, core: 2. Of those that a mesh axis runs over, the one named last changes fastest.
Arguments:
- features: bfloat16 [2, 4, 8, 16, 384], P(None, None, 'rows'), may hold values from -6 to 6
- cache_zero: bfloat16 [2, 2, 8, 16, 384], P(None, None, 'rows'), may hold values from -6 to 6
- cache_one: bfloat16 [2, 2, 16, 32, 384], P(None, None, 'rows'), may hold values from -6 to 6
- cache_two: bfloat16 [2, 2, 32, 64, 384], P(None, None, 'rows'), may hold values from -6 to 6
- cache_three: bfloat16 [2, 2, 64, 128, 192], P(None, None, 'rows'), may hold values from -6 to 6
- gain_zero: float32 [384], replicated, may hold values from 0.4 to 1.6
- gain_one: float32 [384], replicated, may hold values from 0.4 to 1.6
- gain_two: float32 [384], replicated, may hold values from 0.4 to 1.6
- gain_three: float32 [192], replicated, may hold values from 0.4 to 1.6
- weight_zero: bfloat16 [1152, 3, 3, 384], P('rows'), may hold values from -0.0625 to 0.0625
- weight_one: bfloat16 [1152, 3, 3, 384], P('rows'), may hold values from -0.0625 to 0.0625
- weight_two: bfloat16 [1152, 3, 3, 192], P('rows'), may hold values from -0.0625 to 0.0625
- weight_three: bfloat16 [576, 3, 3, 96], P('rows'), may hold values from -0.078125 to 0.078125
- proj_two: bfloat16 [384, 192], replicated, may hold values from -0.3125 to 0.3125
- proj_three: bfloat16 [192, 96], replicated, may hold values from -0.4375 to 0.4375
Outputs:
- decoded: bfloat16 [2, 4, 96, 64, 128], P(None, 'segment', None, 'rows')
The draws below stay inside these ranges and needn't reach their ends.
All inputs are finite; a program needn't handle non-finite values.
Results may differ from the reference program's by a relative error of at most 0.0065.
Values may be sent and summed in bfloat16 or wider, within the bound.
A program may use at most 128 MiB of HBM per device.

```python
import jax
import jax.numpy as jnp
from jax import lax

WIDE = 384
MID = 192
NARROW = 96
VIDEOS = 2
FRAMES = 4
COLS0 = 16
HEIGHT0 = 8
HEIGHT1 = 16
HEIGHT2 = 32
HEIGHT3 = 64
WIDTH1 = 32
WIDTH2 = 64
WIDTH3 = 128


def block_levels(own_key, extent, shards, low, top_value):
    level = 1.0
    for axis_at, blocks in shards:
        draws = jax.random.uniform(jax.random.fold_in(jax.random.fold_in(own_key, 6), axis_at), (blocks,), jnp.float32, low / len(shards), top_value / len(shards))
        level = level * jnp.repeat(jnp.exp(draws), extent[axis_at] // blocks).reshape((-1,) + (1,) * (len(extent) - 1 - axis_at))
    return level


def gaussian(key, shape, spread, bound, split=(), held_as=jnp.bfloat16):
    values = jax.random.normal(key, shape, jnp.float32) * spread
    if len(split) > 0:
        values = block_levels(key, shape, split, -0.22, 0.18) * values
    return jnp.clip(values, min=-bound, max=bound).astype(held_as)


def setup_inputs(seed: int = 0) -> dict:
    streams_of = jax.random.split(jax.random.key(seed), 16)
    features = gaussian(streams_of[0], (VIDEOS, FRAMES, HEIGHT0, COLS0, WIDE), 1.0, 6.0, ((2, 8),))
    cache_zero = gaussian(streams_of[1], (VIDEOS, 2, HEIGHT0, COLS0, WIDE), 1.0, 6.0, ((2, 8),))
    cache_one = gaussian(streams_of[2], (VIDEOS, 2, HEIGHT1, WIDTH1, WIDE), 1.0, 6.0, ((2, 8),))
    cache_two = gaussian(streams_of[3], (VIDEOS, 2, HEIGHT2, WIDTH2, WIDE), 1.0, 6.0, ((2, 8),))
    cache_three = gaussian(streams_of[4], (VIDEOS, 2, HEIGHT3, WIDTH3, MID), 1.0, 6.0, ((2, 8),))
    gain_zero = jnp.clip(1.0 + 0.12 * jax.random.normal(streams_of[5], (WIDE,), jnp.float32), 0.4, 1.6)
    gain_one = jnp.clip(1.0 + 0.12 * jax.random.normal(streams_of[6], (WIDE,), jnp.float32), 0.4, 1.6)
    gain_two = jnp.clip(1.0 + 0.12 * jax.random.normal(streams_of[7], (WIDE,), jnp.float32), 0.4, 1.6)
    gain_three = jnp.clip(1.0 + 0.12 * jax.random.normal(streams_of[8], (MID,), jnp.float32), 0.4, 1.6)
    weight_zero = gaussian(streams_of[9], (3 * WIDE, 3, 3, WIDE), (27 * WIDE) ** -0.5, 0.0625, ((0, 8),))
    weight_one = gaussian(streams_of[10], (3 * WIDE, 3, 3, WIDE), (27 * WIDE) ** -0.5, 0.0625, ((0, 8),))
    weight_two = gaussian(streams_of[11], (3 * WIDE, 3, 3, MID), (27 * WIDE) ** -0.5, 0.0625, ((0, 8),))
    weight_three = gaussian(streams_of[12], (3 * MID, 3, 3, NARROW), (27 * MID) ** -0.5, 0.078125, ((0, 8),))
    proj_two = gaussian(streams_of[13], (WIDE, MID), WIDE ** -0.5, 0.3125)
    proj_three = gaussian(streams_of[14], (MID, NARROW), MID ** -0.5, 0.4375)
    return {"features": features, "cache_zero": cache_zero, "cache_one": cache_one, "cache_two": cache_two, "cache_three": cache_three, "gain_zero": gain_zero, "gain_one": gain_one, "gain_two": gain_two, "gain_three": gain_three, "weight_zero": weight_zero, "weight_one": weight_one, "weight_two": weight_two, "weight_three": weight_three, "proj_two": proj_two, "proj_three": proj_three}


EPSILON = 1e-06

def activate(values, gain_vec):
    widened = values.astype(jnp.float32)
    scaled = widened * lax.rsqrt(lax.optimization_barrier(jnp.mean(widened * widened, axis=-1, keepdims=True)) + EPSILON)
    return jax.nn.silu(scaled * gain_vec.astype(jnp.float32)).astype(jnp.bfloat16)

def enlarge(values):
    return jnp.repeat(jnp.repeat(values, 2, axis=0), 2, axis=1)

def convolve(padded, weight, channels_first):
    frames_in, rows_pad, columns, channels = padded.shape
    height = rows_pad - 2
    wide_pad = jnp.pad(padded, ((0, 0), (0, 0), (1, 1), (0, 0)))
    stacked = jnp.concatenate([wide_pad[:, :, 0:columns], wide_pad[:, :, 1:columns + 1], wide_pad[:, :, 2:columns + 2]], axis=-1)
    summed = None
    for frame_tap in range(3):
        for row_tap in range(3):
            row_block = stacked[frame_tap, row_tap:row_tap + height].reshape(height * columns, 3 * channels)
            if channels_first:
                partial_sum = lax.dot_general(weight[frame_tap, row_tap], row_block, (((0,), (1,)), ((), ())), preferred_element_type=jnp.float32)
            else:
                partial_sum = jnp.dot(row_block, weight[frame_tap, row_tap], preferred_element_type=jnp.float32)
            summed = partial_sum if summed is None else summed + partial_sum
    return summed

def shortcut(segment_in, projection, level):
    flattened = segment_in.reshape(-1, segment_in.shape[-1])
    if level < 2:
        return flattened.astype(jnp.float32)
    if level == 2:
        return jnp.dot(flattened, projection, preferred_element_type=jnp.float32)
    return lax.dot_general(projection, flattened, (((0,), (1,)), ((), ())), preferred_element_type=jnp.float32)

def reference(features, cache_zero, cache_one, cache_two, cache_three, gain_zero, gain_one, gain_two, gain_three, weight_zero, weight_one, weight_two, weight_three, proj_two, proj_three):
    caches = (cache_zero, cache_one, cache_two, cache_three)
    gains = (gain_zero, gain_one, gain_two, gain_three)
    weights = tuple((weight_arr.transpose(1, 2, 0, 3) for weight_arr in (weight_zero, weight_one, weight_two, weight_three)))
    projections = (None, None, proj_two, proj_three)
    videos, frames = (features.shape[0], features.shape[1])
    results = []
    for video_id in range(videos):
        histories = [caches[level][video_id] for level in range(4)]
        outputs = []
        for frame_id in range(frames):
            segment_in = features[video_id, frame_id]
            for level in range(4):
                height, columns = (segment_in.shape[0], segment_in.shape[1])
                newest = activate(segment_in, gains[level])
                window = jnp.concatenate([histories[level], newest[None]], axis=0)
                histories[level] = window[1:]
                padded = jnp.pad(window, ((0, 0), (1, 1), (0, 0), (0, 0)))
                summed = convolve(padded, weights[level], level == 3) + shortcut(segment_in, projections[level], level)
                outcome = summed.astype(jnp.bfloat16)
                out_width = weights[level].shape[-1]
                if level < 3:
                    segment_in = enlarge(outcome.reshape(height, columns, out_width))
                else:
                    outputs.append(outcome.reshape(out_width, height, columns))
        results.append(jnp.stack(outputs))
    return jnp.stack(results)
```

```python
import jax
import jax.numpy as jnp
from jax import lax
from jax.sharding import PartitionSpec as P

EPSILON = 1e-06
BF = jnp.bfloat16
F32 = jnp.float32


def activate(values, gain_vec):
    widened = values.astype(F32)
    scaled = widened * lax.rsqrt(jnp.mean(widened * widened, axis=-1, keepdims=True) + EPSILON)
    return jax.nn.silu(scaled * gain_vec).astype(BF)


def enlarge(values, dim):
    return jnp.repeat(jnp.repeat(values, 2, axis=dim), 2, axis=dim + 1)


def neighbours(array, by):
    size = lax.axis_size("rows")
    up = [(i, i + by) for i in range(size - by)]
    down = [(j, i) for i, j in up]
    return up, down


def from_before(array, by=1):
    size = lax.axis_size("rows")
    return lax.ppermute(array, "rows", [(i, i + by) for i in range(size - by)])


def from_after(array, by=1):
    size = lax.axis_size("rows")
    return lax.ppermute(array, "rows", [(i + by, i) for i in range(size - by)])


def stack_columns(window):
    columns = window.shape[3]
    wide = jnp.pad(window, ((0, 0), (0, 0), (0, 0), (1, 1), (0, 0)))
    return jnp.concatenate(
        [wide[:, :, :, j : j + columns] for j in range(3)], axis=-1
    )


def convolve(window, weight, out_width):
    videos, frames, rows, columns, channels = window.shape
    stacked = stack_columns(window).reshape(-1, 3 * channels)
    product = jnp.dot(stacked, weight, preferred_element_type=F32)
    product = product.reshape(videos, frames, rows, columns, 9 * out_width)
    total = None
    for t in range(3):
        for i in range(3):
            tap = 3 * t + i
            term = product[
                :, t : t + frames - 2, i : i + rows - 2, :, tap * out_width : (tap + 1) * out_width
            ]
            total = term if total is None else total + term
    return total


def shards(
    features,
    cache_zero,
    cache_one,
    cache_two,
    cache_three,
    gain_zero,
    gain_one,
    gain_two,
    gain_three,
    weight_zero,
    weight_one,
    weight_two,
    weight_three,
    proj_two,
    proj_three,
):
    segments = lax.axis_size("segment")
    segment = lax.axis_index("segment")
    row_devices = lax.axis_size("rows")
    row = lax.axis_index("rows")
    frames = features.shape[1]

    def own_channels(array):
        width = array.shape[-1] // segments
        return lax.dynamic_slice_in_dim(array, segment * width, width, array.ndim - 1)

    def gathered(weight):
        return lax.all_gather(
            weight.reshape(weight.shape[0], -1), "rows", axis=0, tiled=True
        )

    full = [
        gathered(own_channels(weight_zero)),
        gathered(own_channels(weight_one)),
        gathered(own_channels(weight_two)),
        gathered(weight_three),
    ]

    def with_rows(array, width):
        rows = array.shape[2]
        before = []
        after = []
        by = 1
        while width > 0:
            take = min(width, rows)
            before.insert(0, from_before(array[:, :, rows - take :], by))
            after.append(from_after(array[:, :, :take], by))
            width -= take
            by += 1
        return jnp.concatenate(before + [array] + after, axis=2)

    def inside(array, halo):
        rows = array.shape[2]
        at = lax.broadcasted_iota(jnp.int32, (1, 1, rows, 1, 1), 2)
        keep = ((at >= halo) | (row > 0)) & ((at < rows - halo) | (row < row_devices - 1))
        return jnp.where(keep, array, jnp.zeros((), array.dtype))

    wide = with_rows(features, 2)
    caches = [
        with_rows(cache_zero, 2),
        with_rows(cache_one, 2),
        with_rows(cache_two, 2),
        with_rows(cache_three, 1),
    ]

    width = weight_zero.shape[3] // segments
    window = jnp.concatenate([caches[0], activate(wide, gain_zero)], axis=1)
    total = convolve(window, full[0], width)
    total = total + own_channels(wide[:, :, 1:-1]).astype(F32)
    mine = inside(total.astype(BF), 1)
    coarse = lax.all_gather(mine, "segment", axis=4, tiled=True)

    width = weight_one.shape[3] // segments
    window = jnp.concatenate([caches[1], enlarge(activate(coarse, gain_one), 2)], axis=1)
    total = convolve(window, full[1], width)
    total = total + enlarge(mine, 2)[:, :, 1:-1].astype(F32)
    mine = inside(total.astype(BF), 1)
    coarse = lax.all_gather(mine, "segment", axis=4, tiled=True)

    width = weight_two.shape[3] // segments
    window = jnp.concatenate([caches[2], enlarge(activate(coarse, gain_two), 2)], axis=1)
    total = convolve(window, full[2], width)
    straight = jnp.dot(
        coarse.reshape(-1, coarse.shape[-1]), own_channels(proj_two), preferred_element_type=F32
    ).reshape(coarse.shape[:-1] + (width,))
    total = total + enlarge(straight, 2)[:, :, 1:-1]
    mine = inside(total.astype(BF), 1)
    coarse = lax.all_gather(mine, "segment", axis=4, tiled=True)

    own = frames // segments
    ahead = jnp.zeros((coarse.shape[0], 2) + coarse.shape[2:], BF)
    recent = lax.dynamic_slice_in_dim(
        jnp.concatenate([ahead, coarse], axis=1), segment * own, own + 2, 1
    )
    newest = enlarge(activate(recent, gain_three), 2)[:, :, 1:-1]
    behind = jnp.pad(caches[3], ((0, 0), (0, frames), (0, 0), (0, 0), (0, 0)))
    behind = lax.dynamic_slice_in_dim(behind, segment * own, own + 2, 1)
    at = segment * own + lax.broadcasted_iota(jnp.int32, (1, own + 2, 1, 1, 1), 1)
    window = jnp.where(at < 2, behind, newest)
    stacked = stack_columns(window)
    videos, _, rows, columns, channels = stacked.shape
    rows -= 2
    out_width = weight_three.shape[3]
    total = None
    for t in range(3):
        for i in range(3):
            tap = 3 * t + i
            block = stacked[:, t : t + own, i : i + rows].reshape(-1, channels)
            term = lax.dot_general(
                full[3][:, tap * out_width : (tap + 1) * out_width],
                block,
                (((0,), (1,)), ((), ())),
                preferred_element_type=F32,
            )
            total = term if total is None else total + term
    mine = recent[:, 2:, 1:-1]
    straight = lax.dot_general(
        proj_three,
        mine.reshape(-1, mine.shape[-1]),
        (((0,), (1,)), ((), ())),
        preferred_element_type=F32,
    ).reshape((out_width,) + mine.shape[:-1])
    total = total.reshape(out_width, videos, own, rows, columns) + enlarge(straight, 3)
    return total.astype(BF).transpose(1, 2, 0, 3, 4)


def solution(mesh):
    slab = P(None, None, "rows", None, None)
    weight = P("rows", None, None, None)
    placed = (slab,) * 5 + (P(),) * 4 + (weight,) * 4 + (P(),) * 2
    return jax.shard_map(
        shards,
        mesh=mesh,
        in_specs=placed,
        out_specs=P(None, "segment", None, "rows", None),
        check_vma=False,
    )
```

```python
import jax
import jax.numpy as jnp
from jax import lax
from jax.experimental import pallas as pl
from jax.experimental.pallas import tpu as pltpu
from jax.sharding import PartitionSpec as P

EPSILON = 1e-06
BF = jnp.bfloat16
F32 = jnp.float32


def activate(values, gain_vec):
    widened = values.astype(F32)
    scaled = widened * lax.rsqrt(jnp.mean(widened * widened, axis=-1, keepdims=True) + EPSILON)
    return jax.nn.silu(scaled * gain_vec).astype(BF)


def enlarge(values, dim):
    return jnp.repeat(jnp.repeat(values, 2, axis=dim), 2, axis=dim + 1)


def from_before(array, by=1):
    size = lax.axis_size("rows")
    return lax.ppermute(array, "rows", [(i, i + by) for i in range(size - by)])


def from_after(array, by=1):
    size = lax.axis_size("rows")
    return lax.ppermute(array, "rows", [(i + by, i) for i in range(size - by)])


def stack_columns(window):
    columns = window.shape[3]
    wide = jnp.pad(window, ((0, 0), (0, 0), (0, 0), (1, 1), (0, 0)))
    return jnp.concatenate(
        [wide[:, :, :, j : j + columns] for j in range(3)], axis=-1
    )


def convolve(window, weight, out_width):
    videos, frames, rows, columns, channels = window.shape
    stacked = stack_columns(window).reshape(-1, 3 * channels)
    product = jnp.dot(stacked, weight, preferred_element_type=F32)
    product = product.reshape(videos, frames, rows, columns, 9 * out_width)
    total = None
    for t in range(3):
        for i in range(3):
            tap = 3 * t + i
            term = product[
                :, t : t + frames - 2, i : i + rows - 2, :, tap * out_width : (tap + 1) * out_width
            ]
            total = term if total is None else total + term
    return total


def selector(rows, columns, offset, fine, transposed=False):
    shape = (columns, rows) if transposed else (rows, columns)
    source = lax.broadcasted_iota(jnp.int32, shape, 1 if transposed else 0) + offset
    at = lax.broadcasted_iota(jnp.int32, shape, 0 if transposed else 1)
    hit = (source == at) if fine else ((source == 2 * at) | (source == 2 * at + 1))
    return jnp.where(hit, 1.0, 0.0).astype(BF)


def picked(a, b):
    return jnp.dot(a, b, preferred_element_type=F32).astype(BF)


def middle_kernel(cache_ref, low_ref, straight_ref, weight_ref, proj_ref, keep_ref, out_ref, stacked, product, plain):
    _, past, rows, columns, channels = cache_ref.shape
    frames = low_ref.shape[1]
    width = proj_ref.shape[1]
    half = columns // 2
    line = rows * columns
    inner = rows - 2
    for j in range(3):
        fine = selector(columns, columns, j - 1, True)
        coarse = selector(columns, half, j - 1, False)
        lanes = slice(j * channels, (j + 1) * channels)

        def old(w, _):
            for q in range(rows):
                at = pl.multiple_of(w * line + q * columns, columns)
                stacked[pl.ds(at, columns), lanes] = picked(fine, cache_ref[0, w, q])
            return 0

        def new(f, _):
            for l in range(rows // 2):
                row = picked(coarse, low_ref[0, f, l])
                at = pl.multiple_of((f + past) * line + 2 * l * columns, columns)
                stacked[pl.ds(at, columns), lanes] = row
                stacked[pl.ds(at + columns, columns), lanes] = row
            return 0

        lax.fori_loop(0, past, old, 0)
        lax.fori_loop(0, frames, new, 0)

    coarse = selector(columns, half, 0, False)

    def multiply(w, _):
        at = pl.multiple_of(w * line, line)
        product[w] = jnp.dot(
            stacked[pl.ds(at, line), :], weight_ref[...], preferred_element_type=F32
        )
        return 0

    lax.fori_loop(0, frames + past, multiply, 0)

    for f in range(frames):
        for q in range(inner):
            plain[q * columns : (q + 1) * columns, :] = picked(
                coarse, straight_ref[0, f, (q + 1) // 2]
            )
        total = jnp.dot(plain[...], proj_ref[...], preferred_element_type=F32)
        for t in range(3):
            for i in range(3):
                tap = 3 * t + i
                total = total + product[
                    f + t,
                    i * columns : (i + inner) * columns,
                    tap * width : (tap + 1) * width,
                ]
        total = jnp.where(keep_ref[...] > 0.0, total, 0.0)
        out_ref[0, :, f * inner * columns : (f + 1) * inner * columns] = total.T.astype(BF)


def middle(cache, low, straight, weight, proj, keep):
    videos, past, rows, columns, channels = cache.shape
    frames = low.shape[1]
    width = proj.shape[1]
    cells = (rows - 2) * columns

    def one(shape):
        return pl.BlockSpec((1,) + shape[1:], lambda v: (v,) + (0,) * (len(shape) - 1))

    def whole(shape):
        return pl.BlockSpec(shape, lambda v: (0,) * len(shape))

    return pl.pallas_call(
        middle_kernel,
        grid=(videos,),
        in_specs=[
            one(cache.shape),
            one(low.shape),
            one(straight.shape),
            whole(weight.shape),
            whole(proj.shape),
            whole(keep.shape),
        ],
        out_specs=one((videos, width, frames * cells)),
        out_shape=jax.ShapeDtypeStruct((videos, width, frames * cells), BF),
        scratch_shapes=[
            pltpu.VMEM(((frames + past) * rows * columns, 3 * channels), BF),
            pltpu.VMEM((frames + past, rows * columns, weight.shape[1]), F32),
            pltpu.VMEM((cells, channels), BF),
        ],
        compiler_params=pltpu.CompilerParams(vmem_limit_bytes=56 * 1024 * 1024),
        name="middle",
    )(cache, low, straight, weight, proj, keep)


def last_kernel(old_ref, cache_ref, low_ref, straight_ref, weight_ref, proj_ref, out_ref, stacked, plain, held):
    videos, taken, rows, channels, columns = cache_ref.shape
    half = columns // 2
    inner = rows - 2

    def spread(offset):
        pair = (2 * half, 2 * columns)
        source = lax.broadcasted_iota(jnp.int32, pair, 1)
        second = source >= columns
        source = jnp.where(second, source - columns, source) + offset
        at = lax.broadcasted_iota(jnp.int32, pair, 0)
        lower = at >= half
        at = jnp.where(lower, at - half, at)
        hit = ((source == 2 * at) | (source == 2 * at + 1)) & (second == lower)
        return jnp.where(hit, 1.0, 0.0).astype(BF)

    def put(t, j, q, value):
        stacked[t, j * channels : (j + 1) * channels, q * columns : (q + 1) * columns] = value

    for t in range(3):
        flag = old_ref[t]

        @pl.when(flag > 0)
        def _():
            for j in range(3):
                fine = selector(columns, columns, j - 1, True, transposed=True)
                for q in range(rows):
                    put(t, j, q, picked(cache_ref[0, t, q], fine))

        @pl.when(flag == 0)
        def _():
            for j in range(3):
                coarse = spread(j - 1)
                for p in range((rows + 2) // 4):
                    at = (t * (rows // 2 + 1) + 2 * p) * half
                    both = picked(low_ref[0, :, at : at + 2 * half], coarse)
                    for part in range(2):
                        for q in (4 * p + 2 * part - 1, 4 * p + 2 * part):
                            if 0 <= q < rows:
                                put(t, j, q, both[:, part * columns : (part + 1) * columns])

    coarse = spread(0)
    for p in range((rows + 2) // 4):
        at = 2 * p * half
        both = picked(straight_ref[0, :, at : at + 2 * half], coarse)
        for part in range(2):
            for q in (4 * p + 2 * part - 1, 4 * p + 2 * part):
                if 1 <= q <= inner:
                    plain[:, (q - 1) * columns : q * columns] = both[
                        :, part * columns : (part + 1) * columns
                    ]

    total = jnp.dot(proj_ref[...], plain[...], preferred_element_type=F32)
    for t in range(3):
        for i in range(3):
            total = total + jnp.dot(
                weight_ref[3 * t + i],
                stacked[t, :, i * columns : (i + inner) * columns],
                preferred_element_type=F32,
            )
    for q in range(inner):
        held[:, q, :] = total[:, q * columns : (q + 1) * columns]
    out_ref[0, 0] = held[...].astype(BF)


def last(old, cache, low, straight, weight, proj):
    videos, taken, rows, channels, columns = cache.shape
    width = proj.shape[0]

    def one(shape):
        return pl.BlockSpec((1,) + shape[1:], lambda v, old: (v,) + (0,) * (len(shape) - 1))

    def whole(shape):
        return pl.BlockSpec(shape, lambda v, old: (0,) * len(shape))

    out = (videos, 1, width, rows - 2, columns)
    return pl.pallas_call(
        last_kernel,
        grid_spec=pltpu.PrefetchScalarGridSpec(
            num_scalar_prefetch=1,
            grid=(videos,),
            in_specs=[
                one(cache.shape),
                one(low.shape),
                one(straight.shape),
                whole(weight.shape),
                whole(proj.shape),
            ],
            out_specs=one(out),
            scratch_shapes=[
                pltpu.VMEM((3, 3 * channels, rows * columns), BF),
                pltpu.VMEM((channels, (rows - 2) * columns), BF),
                pltpu.VMEM((width, rows - 2, columns), F32),
            ],
        ),
        out_shape=jax.ShapeDtypeStruct(out, BF),
        compiler_params=pltpu.CompilerParams(vmem_limit_bytes=56 * 1024 * 1024),
        name="last",
    )(old, cache, low, straight, weight, proj)


def shards(
    features,
    cache_zero,
    cache_one,
    cache_two,
    cache_three,
    gain_zero,
    gain_one,
    gain_two,
    gain_three,
    weight_zero,
    weight_one,
    weight_two,
    weight_three,
    proj_two,
    proj_three,
):
    segments = lax.axis_size("segment")
    segment = lax.axis_index("segment")
    row_devices = lax.axis_size("rows")
    row = lax.axis_index("rows")
    frames = features.shape[1]

    def own_channels(array):
        width = array.shape[-1] // segments
        return lax.dynamic_slice_in_dim(array, segment * width, width, array.ndim - 1)

    def gathered(weight):
        return lax.all_gather(
            weight.reshape(weight.shape[0], -1), "rows", axis=0, tiled=True
        )

    full = [
        gathered(own_channels(weight_zero)),
        gathered(own_channels(weight_one)),
        gathered(own_channels(weight_two)),
        gathered(weight_three),
    ]

    def with_rows(array, width):
        rows = array.shape[2]
        before = []
        after = []
        by = 1
        while width > 0:
            take = min(width, rows)
            before.insert(0, from_before(array[:, :, rows - take :], by))
            after.append(from_after(array[:, :, :take], by))
            width -= take
            by += 1
        return jnp.concatenate(before + [array] + after, axis=2)

    def inside(array, halo):
        rows = array.shape[2]
        at = lax.broadcasted_iota(jnp.int32, (1, 1, rows, 1, 1), 2)
        keep = ((at >= halo) | (row > 0)) & ((at < rows - halo) | (row < row_devices - 1))
        return jnp.where(keep, array, jnp.zeros((), array.dtype))

    wide = with_rows(features, 2)
    caches = [
        with_rows(cache_zero, 2),
        with_rows(cache_one, 2),
        with_rows(cache_two, 2),
        with_rows(cache_three, 1),
    ]

    width = weight_zero.shape[3] // segments
    window = jnp.concatenate([caches[0], activate(wide, gain_zero)], axis=1)
    total = convolve(window, full[0], width)
    total = total + own_channels(wide[:, :, 1:-1]).astype(F32)
    mine = inside(total.astype(BF), 1)
    coarse = lax.all_gather(mine, "segment", axis=4, tiled=True)

    width = weight_one.shape[3] // segments
    window = jnp.concatenate([caches[1], enlarge(activate(coarse, gain_one), 2)], axis=1)
    total = convolve(window, full[1], width)
    total = total + enlarge(mine, 2)[:, :, 1:-1].astype(F32)
    mine = inside(total.astype(BF), 1)
    coarse = lax.all_gather(mine, "segment", axis=4, tiled=True)

    width = weight_two.shape[3] // segments
    rows = caches[2].shape[2] - 2
    columns = caches[2].shape[3]
    at = lax.broadcasted_iota(jnp.int32, (rows * columns, 1), 0) // columns
    keep = ((at >= 1) | (row > 0)) & ((at < rows - 1) | (row < row_devices - 1))
    mine = middle(
        caches[2],
        activate(coarse, gain_two),
        coarse,
        full[2],
        own_channels(proj_two),
        keep.astype(F32),
    )
    coarse = lax.all_gather(mine, "segment", axis=1, tiled=True)

    own = frames // segments
    videos, channels = coarse.shape[:2]
    cells = rows * columns
    ahead = jnp.zeros((videos, channels, 2 * cells), BF)
    recent = lax.dynamic_slice_in_dim(
        jnp.concatenate([ahead, coarse], axis=2), segment * own * cells, (own + 2) * cells, 2
    )
    widened = recent.astype(F32)
    widened = widened * lax.rsqrt(
        jnp.mean(widened * widened, axis=1, keepdims=True) + EPSILON
    )
    newest = jax.nn.silu(widened * gain_three[:, None]).astype(BF)
    behind = caches[3].transpose(0, 1, 2, 4, 3)
    behind = jnp.pad(behind, ((0, 0), (0, own), (0, 0), (0, 0), (0, 0)))
    swapped = jnp.concatenate([behind[:, 1:2], behind[:, 2:3], behind[:, 2:3]], axis=1)
    behind = jnp.where(segment * own == 0, behind, swapped)
    old = (segment * own + jnp.arange(own + 2, dtype=jnp.int32) < 2).astype(jnp.int32)
    taps = full[3].reshape(full[3].shape[0], 9, -1).transpose(1, 2, 0)
    return last(old, behind, newest, recent[:, :, 2 * cells :], taps, proj_three.T)


def solution(mesh):
    slab = P(None, None, "rows", None, None)
    weight = P("rows", None, None, None)
    placed = (slab,) * 5 + (P(),) * 4 + (weight,) * 4 + (P(),) * 2
    return jax.shard_map(
        shards,
        mesh=mesh,
        in_specs=placed,
        out_specs=P(None, "segment", None, "rows", None),
        check_vma=False,
    )
```

```python
import functools

import jax
import jax.numpy as jnp
from jax import lax
from jax.experimental import pallas as pl
from jax.experimental.pallas import tpu as pltpu
from jax.sharding import PartitionSpec as P

EPSILON = 1e-06
BF = jnp.bfloat16
F32 = jnp.float32


def activate(values, gain_vec):
    widened = values.astype(F32)
    scaled = widened * lax.rsqrt(jnp.mean(widened * widened, axis=-1, keepdims=True) + EPSILON)
    return jax.nn.silu(scaled * gain_vec).astype(BF)


def enlarge(values, dim):
    return jnp.repeat(jnp.repeat(values, 2, axis=dim), 2, axis=dim + 1)


MESH = pl.DeviceIdType.MESH


def ring_place(row, size):
    return jnp.where(row % 2 == 0, row // 2, size - 1 - row // 2)


def ring_row(place, size):
    return jnp.where(place < size // 2, 2 * place, 2 * (size - 1 - place) + 1)


def halo_plan(shapes, widths):
    plan = []
    for k, (shape, width) in enumerate(zip(shapes, widths)):
        by = 1
        while width > 0:
            take = min(width, shape[2])
            plan.append((k, by, take))
            width -= take
            by += 1
    return plan


def collect_kernel(size, weights, slabs, plan, *refs):
    shards = refs[:weights]
    edges = refs[weights : weights + slabs]
    refs = refs[weights + slabs :]
    whole = refs[:weights]
    halos = refs[weights : weights + 2 * len(plan)]
    send, recv, own, edge_send, edge_recv = refs[weights + 2 * len(plan) :]
    row = lax.axis_index("rows")
    place = ring_place(row, size)
    ahead = ring_row((place + 1) % size, size)
    back = ring_row((place + size - 1) % size, size)
    far = max(by for _, by, _ in plan)

    barrier = pltpu.get_barrier_semaphore()
    pl.semaphore_signal(barrier, inc=1, device_id={"rows": ahead}, device_id_type=MESH)
    pl.semaphore_signal(barrier, inc=1, device_id={"rows": back}, device_id_type=MESH)
    for by in range(1, far + 1):

        @pl.when(row + by < size)
        def _():
            pl.semaphore_signal(barrier, inc=1, device_id={"rows": row + by}, device_id_type=MESH)

        @pl.when(row >= by)
        def _():
            pl.semaphore_signal(barrier, inc=1, device_id={"rows": row - by}, device_id_type=MESH)

    peers = 2 + jnp.minimum(row, far) + jnp.minimum(size - 1 - row, far)
    pl.semaphore_wait(barrier, peers)

    def hop(k, way, step):
        origin = (place + size - step) % size if way == 0 else (place + step) % size
        origin = ring_row(origin, size)
        return pltpu.make_async_remote_copy(
            src_ref=shards[k] if step == 0 else whole[k].at[origin],
            dst_ref=whole[k].at[origin],
            send_sem=send.at[k, way, step],
            recv_sem=recv.at[k, way, step],
            device_id={"rows": ahead if way == 0 else back},
            device_id_type=MESH,
        )

    def edge(n, way):
        k, by, take = plan[n]
        rows = edges[k].shape[2]
        first = rows - take if way == 0 else 0
        other = row + by if way == 0 else row - by
        return pltpu.make_async_remote_copy(
            src_ref=edges[k].at[:, :, first : first + take],
            dst_ref=halos[2 * n + way],
            send_sem=edge_send.at[n, way],
            recv_sem=edge_recv.at[n, way],
            device_id={"rows": jnp.clip(other, 0, size - 1)},
            device_id_type=MESH,
        )

    steps = (size // 2, size - 1 - size // 2)
    local = []
    for k in range(weights):
        for way in range(2):
            if steps[way] > 0:
                hop(k, way, 0).start()
        copy = pltpu.make_async_copy(shards[k], whole[k].at[row], own.at[k])
        copy.start()
        local.append(copy)
    for n, (_, by, _) in enumerate(plan):

        @pl.when(row + by < size)
        def _():
            edge(n, 0).start()

        @pl.when(row >= by)
        def _():
            edge(n, 1).start()

    for step in range(steps[0]):
        for k in range(weights):
            for way in range(2):
                if step < steps[way]:
                    hop(k, way, step).wait_recv()
                    if step + 1 < steps[way]:
                        hop(k, way, step + 1).start()
    for k in range(weights):
        local[k].wait()
        for way in range(2):
            for step in range(steps[way]):
                hop(k, way, step).wait_send()
    for n, (_, by, _) in enumerate(plan):

        @pl.when(row + by < size)
        def _():
            edge(n, 0).wait_send()
            edge(n, 1).wait_recv()

        @pl.when(row >= by)
        def _():
            edge(n, 1).wait_send()
            edge(n, 0).wait_recv()


def collect(weights, slabs, widths):
    size = lax.axis_size("rows")
    plan = halo_plan([slab.shape for slab in slabs], widths)
    out = [jax.ShapeDtypeStruct((size,) + w.shape, w.dtype) for w in weights]
    for k, _, take in plan:
        shape = slabs[k].shape
        out += [jax.ShapeDtypeStruct(shape[:2] + (take,) + shape[3:], BF)] * 2
    count = len(weights)
    anywhere = pl.BlockSpec(memory_space=pl.ANY)
    got = pl.pallas_call(
        functools.partial(collect_kernel, size, count, len(slabs), plan),
        in_specs=[anywhere] * (count + len(slabs)),
        out_specs=[anywhere] * len(out),
        out_shape=out,
        scratch_shapes=[
            pltpu.SemaphoreType.DMA((count, 2, size // 2 + 1)),
            pltpu.SemaphoreType.DMA((count, 2, size // 2 + 1)),
            pltpu.SemaphoreType.DMA((count,)),
            pltpu.SemaphoreType.DMA((len(plan), 2)),
            pltpu.SemaphoreType.DMA((len(plan), 2)),
        ],
        compiler_params=pltpu.CompilerParams(collective_id=0, has_side_effects=True),
        name="collect",
    )(*weights, *slabs)
    full = [w.reshape((-1,) + w.shape[2:]) for w in got[:count]]
    row = lax.axis_index("rows")
    wide = []
    for k, slab in enumerate(slabs):
        before, after = [], []
        for n, (at, by, _) in enumerate(plan):
            if at == k:
                zero = jnp.zeros((), BF)
                before.insert(0, jnp.where(row >= by, got[count + 2 * n], zero))
                after.append(jnp.where(row + by < size, got[count + 2 * n + 1], zero))
        wide.append(jnp.concatenate(before + [slab] + after, axis=2))
    return full, wide


def across_kernel(size, mine_ref, out_ref, send, recv, own):
    me = lax.axis_index("segment")
    twin = me + 1 - 2 * (me % 2)
    chips = size // 2
    others = [(me + 2 * k) % size for k in range(1, chips)]
    barrier = pltpu.get_barrier_semaphore()
    for other in [twin] + others:
        pl.semaphore_signal(barrier, inc=1, device_id={"segment": other}, device_id_type=MESH)
    pl.semaphore_wait(barrier, chips)

    def copy(n, source, slot, other):
        return pltpu.make_async_remote_copy(
            src_ref=source,
            dst_ref=out_ref.at[slot],
            send_sem=send.at[n],
            recv_sem=recv.at[n],
            device_id={"segment": other},
            device_id_type=MESH,
        )

    far = [copy(k, mine_ref, me, other) for k, other in enumerate(others)]
    for one in far:
        one.start()
    near = copy(chips - 1, mine_ref, me, twin)
    near.start()
    keep = pltpu.make_async_copy(mine_ref, out_ref.at[me], own.at[0])
    keep.start()
    passed = []
    for k in range(1, chips):
        far[k - 1].wait_recv()
        origin = (me + size - 2 * k) % size
        on = copy(chips - 1 + k, out_ref.at[origin], origin, twin)
        on.start()
        passed.append(on)
    for one in far:
        one.wait_send()
    near.wait()
    for on in passed:
        on.wait()
    keep.wait()


def across(mine, number):
    size = lax.axis_size("segment")
    count = 2 * (size // 2) - 1
    return pl.pallas_call(
        functools.partial(across_kernel, size),
        in_specs=[pl.BlockSpec(memory_space=pltpu.VMEM)],
        out_specs=pl.BlockSpec(memory_space=pltpu.VMEM),
        out_shape=jax.ShapeDtypeStruct((size,) + mine.shape, mine.dtype),
        scratch_shapes=[
            pltpu.SemaphoreType.DMA((count,)),
            pltpu.SemaphoreType.DMA((count,)),
            pltpu.SemaphoreType.DMA((1,)),
        ],
        compiler_params=pltpu.CompilerParams(collective_id=number, has_side_effects=True),
        name="across",
    )(mine)


def stack_columns(window):
    columns = window.shape[3]
    wide = jnp.pad(window, ((0, 0), (0, 0), (0, 0), (1, 1), (0, 0)))
    return jnp.concatenate(
        [wide[:, :, :, j : j + columns] for j in range(3)], axis=-1
    )


def convolve(window, weight, out_width):
    videos, frames, rows, columns, channels = window.shape
    stacked = stack_columns(window).reshape(-1, 3 * channels)
    product = jnp.dot(stacked, weight, preferred_element_type=F32)
    product = product.reshape(videos, frames, rows, columns, 9 * out_width)
    total = None
    for t in range(3):
        for i in range(3):
            tap = 3 * t + i
            term = product[
                :, t : t + frames - 2, i : i + rows - 2, :, tap * out_width : (tap + 1) * out_width
            ]
            total = term if total is None else total + term
    return total


def selector(rows, columns, offset, fine, transposed=False):
    shape = (columns, rows) if transposed else (rows, columns)
    source = lax.broadcasted_iota(jnp.int32, shape, 1 if transposed else 0) + offset
    at = lax.broadcasted_iota(jnp.int32, shape, 0 if transposed else 1)
    hit = (source == at) if fine else ((source == 2 * at) | (source == 2 * at + 1))
    return jnp.where(hit, 1.0, 0.0).astype(BF)


def picked(a, b):
    return jnp.dot(a, b, preferred_element_type=F32).astype(BF)


def middle_kernel(cache_ref, low_ref, straight_ref, weight_ref, proj_ref, keep_ref, out_ref, stacked, product, plain):
    _, past, rows, columns, channels = cache_ref.shape
    frames = low_ref.shape[1]
    width = proj_ref.shape[1]
    half = columns // 2
    line = rows * columns
    inner = rows - 2
    for j in range(3):
        fine = selector(columns, columns, j - 1, True)
        coarse = selector(columns, half, j - 1, False)
        lanes = slice(j * channels, (j + 1) * channels)

        def old(w, _):
            for q in range(rows):
                at = pl.multiple_of(w * line + q * columns, columns)
                stacked[pl.ds(at, columns), lanes] = picked(fine, cache_ref[0, w, q])
            return 0

        def new(f, _):
            for l in range(rows // 2):
                row = picked(coarse, low_ref[0, f, l])
                at = pl.multiple_of((f + past) * line + 2 * l * columns, columns)
                stacked[pl.ds(at, columns), lanes] = row
                stacked[pl.ds(at + columns, columns), lanes] = row
            return 0

        lax.fori_loop(0, past, old, 0)
        lax.fori_loop(0, frames, new, 0)

    coarse = selector(columns, half, 0, False)

    def multiply(w, _):
        at = pl.multiple_of(w * line, line)
        product[w] = jnp.dot(
            stacked[pl.ds(at, line), :], weight_ref[...], preferred_element_type=F32
        )
        return 0

    lax.fori_loop(0, frames + past, multiply, 0)

    for f in range(frames):
        for q in range(inner):
            plain[q * columns : (q + 1) * columns, :] = picked(
                coarse, straight_ref[0, f, (q + 1) // 2]
            )
        total = jnp.dot(plain[...], proj_ref[...], preferred_element_type=F32)
        for t in range(3):
            for i in range(3):
                tap = 3 * t + i
                total = total + product[
                    f + t,
                    i * columns : (i + inner) * columns,
                    tap * width : (tap + 1) * width,
                ]
        total = jnp.where(keep_ref[...] > 0.0, total, 0.0)
        out_ref[0, :, f * inner * columns : (f + 1) * inner * columns] = total.T.astype(BF)


def middle(cache, low, straight, weight, proj, keep):
    videos, past, rows, columns, channels = cache.shape
    frames = low.shape[1]
    width = proj.shape[1]
    cells = (rows - 2) * columns

    def one(shape):
        return pl.BlockSpec((1,) + shape[1:], lambda v: (v,) + (0,) * (len(shape) - 1))

    def whole(shape):
        return pl.BlockSpec(shape, lambda v: (0,) * len(shape))

    return pl.pallas_call(
        middle_kernel,
        grid=(videos,),
        in_specs=[
            one(cache.shape),
            one(low.shape),
            one(straight.shape),
            whole(weight.shape),
            whole(proj.shape),
            whole(keep.shape),
        ],
        out_specs=one((videos, width, frames * cells)),
        out_shape=jax.ShapeDtypeStruct((videos, width, frames * cells), BF),
        scratch_shapes=[
            pltpu.VMEM(((frames + past) * rows * columns, 3 * channels), BF),
            pltpu.VMEM((frames + past, rows * columns, weight.shape[1]), F32),
            pltpu.VMEM((cells, channels), BF),
        ],
        compiler_params=pltpu.CompilerParams(vmem_limit_bytes=56 * 1024 * 1024),
        name="middle",
    )(cache, low, straight, weight, proj, keep)


def last_kernel(old_ref, cache_ref, low_ref, straight_ref, weight_ref, proj_ref, out_ref, stacked, plain, held):
    videos, taken, rows, channels, columns = cache_ref.shape
    half = columns // 2
    inner = rows - 2

    def spread(offset):
        pair = (2 * half, 2 * columns)
        source = lax.broadcasted_iota(jnp.int32, pair, 1)
        second = source >= columns
        source = jnp.where(second, source - columns, source) + offset
        at = lax.broadcasted_iota(jnp.int32, pair, 0)
        lower = at >= half
        at = jnp.where(lower, at - half, at)
        hit = ((source == 2 * at) | (source == 2 * at + 1)) & (second == lower)
        return jnp.where(hit, 1.0, 0.0).astype(BF)

    def put(t, j, q, value):
        stacked[t, j * channels : (j + 1) * channels, q * columns : (q + 1) * columns] = value

    for t in range(3):
        flag = old_ref[t]

        @pl.when(flag > 0)
        def _():
            for j in range(3):
                fine = selector(columns, columns, j - 1, True, transposed=True)
                for q in range(rows):
                    put(t, j, q, picked(cache_ref[0, t, q], fine))

        @pl.when(flag == 0)
        def _():
            for j in range(3):
                coarse = spread(j - 1)
                for p in range((rows + 2) // 4):
                    at = (t * (rows // 2 + 1) + 2 * p) * half
                    both = picked(low_ref[0, :, at : at + 2 * half], coarse)
                    for part in range(2):
                        for q in (4 * p + 2 * part - 1, 4 * p + 2 * part):
                            if 0 <= q < rows:
                                put(t, j, q, both[:, part * columns : (part + 1) * columns])

    coarse = spread(0)
    for p in range((rows + 2) // 4):
        at = 2 * p * half
        both = picked(straight_ref[0, :, at : at + 2 * half], coarse)
        for part in range(2):
            for q in (4 * p + 2 * part - 1, 4 * p + 2 * part):
                if 1 <= q <= inner:
                    plain[:, (q - 1) * columns : q * columns] = both[
                        :, part * columns : (part + 1) * columns
                    ]

    total = jnp.dot(proj_ref[...], plain[...], preferred_element_type=F32)
    for t in range(3):
        for i in range(3):
            total = total + jnp.dot(
                weight_ref[3 * t + i],
                stacked[t, :, i * columns : (i + inner) * columns],
                preferred_element_type=F32,
            )
    for q in range(inner):
        held[:, q, :] = total[:, q * columns : (q + 1) * columns]
    out_ref[0, 0] = held[...].astype(BF)


def last(old, cache, low, straight, weight, proj):
    videos, taken, rows, channels, columns = cache.shape
    width = proj.shape[0]

    def one(shape):
        return pl.BlockSpec((1,) + shape[1:], lambda v, old: (v,) + (0,) * (len(shape) - 1))

    def whole(shape):
        return pl.BlockSpec(shape, lambda v, old: (0,) * len(shape))

    out = (videos, 1, width, rows - 2, columns)
    return pl.pallas_call(
        last_kernel,
        grid_spec=pltpu.PrefetchScalarGridSpec(
            num_scalar_prefetch=1,
            grid=(videos,),
            in_specs=[
                one(cache.shape),
                one(low.shape),
                one(straight.shape),
                whole(weight.shape),
                whole(proj.shape),
            ],
            out_specs=one(out),
            scratch_shapes=[
                pltpu.VMEM((3, 3 * channels, rows * columns), BF),
                pltpu.VMEM((channels, (rows - 2) * columns), BF),
                pltpu.VMEM((width, rows - 2, columns), F32),
            ],
        ),
        out_shape=jax.ShapeDtypeStruct(out, BF),
        compiler_params=pltpu.CompilerParams(vmem_limit_bytes=56 * 1024 * 1024),
        name="last",
    )(old, cache, low, straight, weight, proj)


def shards(
    features,
    cache_zero,
    cache_one,
    cache_two,
    cache_three,
    gain_zero,
    gain_one,
    gain_two,
    gain_three,
    weight_zero,
    weight_one,
    weight_two,
    weight_three,
    proj_two,
    proj_three,
):
    segments = lax.axis_size("segment")
    segment = lax.axis_index("segment")
    row_devices = lax.axis_size("rows")
    row = lax.axis_index("rows")
    frames = features.shape[1]

    def own_channels(array):
        width = array.shape[-1] // segments
        return lax.dynamic_slice_in_dim(array, segment * width, width, array.ndim - 1)

    def flat(weight):
        return weight.reshape(weight.shape[0], -1)

    full, slabs = collect(
        [
            flat(own_channels(weight_zero)),
            flat(own_channels(weight_one)),
            flat(own_channels(weight_two)),
            flat(weight_three),
        ],
        [features, cache_zero, cache_one, cache_two, cache_three.transpose(0, 1, 2, 4, 3)],
        [2, 2, 2, 2, 1],
    )
    wide = slabs[0]
    caches = slabs[1:]

    def channels_joined(blocks):
        return jnp.concatenate([blocks[k] for k in range(segments)], axis=-1)

    def inside(array, halo):
        rows = array.shape[2]
        at = lax.broadcasted_iota(jnp.int32, (1, 1, rows, 1, 1), 2)
        keep = ((at >= halo) | (row > 0)) & ((at < rows - halo) | (row < row_devices - 1))
        return jnp.where(keep, array, jnp.zeros((), array.dtype))

    width = weight_zero.shape[3] // segments
    window = jnp.concatenate([caches[0], activate(wide, gain_zero)], axis=1)
    total = convolve(window, full[0], width)
    total = total + own_channels(wide[:, :, 1:-1]).astype(F32)
    mine = inside(total.astype(BF), 1)
    coarse = channels_joined(across(mine, 1))

    width = weight_one.shape[3] // segments
    window = jnp.concatenate([caches[1], enlarge(activate(coarse, gain_one), 2)], axis=1)
    total = convolve(window, full[1], width)
    total = total + enlarge(mine, 2)[:, :, 1:-1].astype(F32)
    mine = inside(total.astype(BF), 1)
    coarse = channels_joined(across(mine, 2))

    width = weight_two.shape[3] // segments
    rows = caches[2].shape[2] - 2
    columns = caches[2].shape[3]
    at = lax.broadcasted_iota(jnp.int32, (rows * columns, 1), 0) // columns
    keep = ((at >= 1) | (row > 0)) & ((at < rows - 1) | (row < row_devices - 1))
    mine = middle(
        caches[2],
        activate(coarse, gain_two),
        coarse,
        full[2],
        own_channels(proj_two),
        keep.astype(F32),
    )
    coarse = jnp.concatenate([blocks for blocks in across(mine, 3)], axis=1)

    own = frames // segments
    videos, channels = coarse.shape[:2]
    cells = rows * columns
    ahead = jnp.zeros((videos, channels, 2 * cells), BF)
    recent = lax.dynamic_slice_in_dim(
        jnp.concatenate([ahead, coarse], axis=2), segment * own * cells, (own + 2) * cells, 2
    )
    widened = recent.astype(F32)
    widened = widened * lax.rsqrt(
        jnp.mean(widened * widened, axis=1, keepdims=True) + EPSILON
    )
    newest = jax.nn.silu(widened * gain_three[:, None]).astype(BF)
    behind = caches[3]
    behind = jnp.pad(behind, ((0, 0), (0, own), (0, 0), (0, 0), (0, 0)))
    swapped = jnp.concatenate([behind[:, 1:2], behind[:, 2:3], behind[:, 2:3]], axis=1)
    behind = jnp.where(segment * own == 0, behind, swapped)
    old = (segment * own + jnp.arange(own + 2, dtype=jnp.int32) < 2).astype(jnp.int32)
    taps = full[3].reshape(full[3].shape[0], 9, -1).transpose(1, 2, 0)
    return last(old, behind, newest, recent[:, :, 2 * cells :], taps, proj_three.T)


def solution(mesh):
    slab = P(None, None, "rows", None, None)
    weight = P("rows", None, None, None)
    placed = (slab,) * 5 + (P(),) * 4 + (weight,) * 4 + (P(),) * 2
    return jax.shard_map(
        shards,
        mesh=mesh,
        in_specs=placed,
        out_specs=P(None, "segment", None, "rows", None),
        check_vma=False,
    )
```

```python
import functools

import jax
import jax.numpy as jnp
from jax import lax
from jax.experimental import pallas as pl
from jax.experimental.pallas import tpu as pltpu
from jax.sharding import PartitionSpec as P

EPSILON = 1e-06
BF = jnp.bfloat16
F32 = jnp.float32


def activate(values, gain_vec):
    widened = values.astype(F32)
    scaled = widened * lax.rsqrt(jnp.mean(widened * widened, axis=-1, keepdims=True) + EPSILON)
    return jax.nn.silu(scaled * gain_vec).astype(BF)


def enlarge(values, dim):
    return jnp.repeat(jnp.repeat(values, 2, axis=dim), 2, axis=dim + 1)


MESH = pl.DeviceIdType.MESH


def ring_place(row, size):
    return jnp.where(row % 2 == 0, row // 2, size - 1 - row // 2)


def ring_row(place, size):
    return jnp.where(place < size // 2, 2 * place, 2 * (size - 1 - place) + 1)


def halo_plan(shapes, widths):
    plan = []
    for k, (shape, width) in enumerate(zip(shapes, widths)):
        by = 1
        while width > 0:
            take = min(width, shape[2])
            plan.append((k, by, take))
            width -= take
            by += 1
    return plan


def collect_kernel(size, weights, slabs, plan, *refs):
    shards = refs[:weights]
    edges = refs[weights : weights + slabs]
    refs = refs[weights + slabs :]
    whole = refs[:weights]
    halos = refs[weights : weights + 2 * len(plan)]
    send, recv, own, edge_send, edge_recv, pass_send, pass_recv = refs[weights + 2 * len(plan) :]
    row = lax.axis_index("rows")
    core = lax.axis_index("segment") % 2
    twin = lax.axis_index("segment") + 1 - 2 * core
    place = ring_place(row, size)
    ahead = ring_row((place + 1) % size, size)
    back = ring_row((place + size - 1) % size, size)
    far = max(by for _, by, _ in plan)

    barrier = pltpu.get_barrier_semaphore()
    pl.semaphore_signal(barrier, inc=1, device_id={"rows": ahead}, device_id_type=MESH)
    pl.semaphore_signal(barrier, inc=1, device_id={"rows": back}, device_id_type=MESH)
    pl.semaphore_signal(barrier, inc=1, device_id={"segment": twin}, device_id_type=MESH)
    for by in range(1, far + 1):

        @pl.when(row + by < size)
        def _():
            pl.semaphore_signal(barrier, inc=1, device_id={"rows": row + by}, device_id_type=MESH)

        @pl.when(row >= by)
        def _():
            pl.semaphore_signal(barrier, inc=1, device_id={"rows": row - by}, device_id_type=MESH)

    peers = 3 + jnp.minimum(row, far) + jnp.minimum(size - 1 - row, far)
    pl.semaphore_wait(barrier, peers)

    def hop(k, way, step):
        origin = (place + size - step) % size if way == 0 else (place + step) % size
        origin = ring_row(origin, size)
        return pltpu.make_async_remote_copy(
            src_ref=shards[k] if step == 0 else whole[k].at[origin],
            dst_ref=whole[k].at[origin],
            send_sem=send.at[k, way, step],
            recv_sem=recv.at[k, way, step],
            device_id={"rows": ahead if way == 0 else back},
            device_id_type=MESH,
        )

    def edge(n, way):
        k, by, take = plan[n]
        rows = edges[k].shape[2]
        first = rows - take if way == 0 else 0
        other = row + by if way == 0 else row - by
        return pltpu.make_async_remote_copy(
            src_ref=edges[k].at[:, :, first : first + take],
            dst_ref=halos[2 * n + way],
            send_sem=edge_send.at[n, way],
            recv_sem=edge_recv.at[n, way],
            device_id={"rows": jnp.clip(other, 0, size - 1)},
            device_id_type=MESH,
        )

    def pass_on(n, way):
        return pltpu.make_async_remote_copy(
            src_ref=halos[2 * n + way],
            dst_ref=halos[2 * n + way],
            send_sem=pass_send.at[n, way],
            recv_sem=pass_recv.at[n, way],
            device_id={"segment": twin},
            device_id_type=MESH,
        )

    def steps(k, way):
        return size // 2 - (way != min(k % 3, 1))

    def each_edge(action):
        for n, (_, by, _) in enumerate(plan):
            above, below = row >= by, row + by < size
            action(n, 0, below, above, core == n % 2)
            action(n, 1, above, below, core == (n + 1) % 2)

    def start(n, way, sends, receives, mine):
        @pl.when(sends & mine)
        def _():
            edge(n, way).start()

    def relay(n, way, sends, receives, mine):
        @pl.when(receives & mine)
        def _():
            edge(n, way).wait_recv()
            pass_on(n, way).start()

    def finish(n, way, sends, receives, mine):
        @pl.when(sends & mine)
        def _():
            edge(n, way).wait_send()

        @pl.when(receives & mine)
        def _():
            pass_on(n, way).wait_send()

        @pl.when(receives & jnp.logical_not(mine))
        def _():
            pass_on(n, way).wait_recv()

    local = []
    for k in range(weights):
        for way in range(2):
            if steps(k, way) > 0:
                hop(k, way, 0).start()
        copy = pltpu.make_async_copy(shards[k], whole[k].at[row], own.at[k])
        copy.start()
        local.append(copy)
    each_edge(start)
    for step in range(size // 2):
        for k in range(weights):
            for way in range(2):
                if step < steps(k, way):
                    hop(k, way, step).wait_recv()
                    if step + 1 < steps(k, way):
                        hop(k, way, step + 1).start()
        if step == size // 2 - 2:
            each_edge(relay)
    if size // 2 < 2:
        each_edge(relay)
    for k in range(weights):
        local[k].wait()
        for way in range(2):
            for step in range(steps(k, way)):
                hop(k, way, step).wait_send()
    each_edge(finish)


def collect(weights, slabs, widths):
    size = lax.axis_size("rows")
    plan = halo_plan([slab.shape for slab in slabs], widths)
    out = [jax.ShapeDtypeStruct((size,) + w.shape, w.dtype) for w in weights]
    for k, _, take in plan:
        shape = slabs[k].shape
        out += [jax.ShapeDtypeStruct(shape[:2] + (take,) + shape[3:], BF)] * 2
    count = len(weights)
    anywhere = pl.BlockSpec(memory_space=pl.ANY)
    got = pl.pallas_call(
        functools.partial(collect_kernel, size, count, len(slabs), plan),
        in_specs=[anywhere] * (count + len(slabs)),
        out_specs=[anywhere] * len(out),
        out_shape=out,
        scratch_shapes=[
            pltpu.SemaphoreType.DMA((count, 2, size // 2 + 1)),
            pltpu.SemaphoreType.DMA((count, 2, size // 2 + 1)),
            pltpu.SemaphoreType.DMA((count,)),
            pltpu.SemaphoreType.DMA((len(plan), 2)),
            pltpu.SemaphoreType.DMA((len(plan), 2)),
            pltpu.SemaphoreType.DMA((len(plan), 2)),
            pltpu.SemaphoreType.DMA((len(plan), 2)),
        ],
        compiler_params=pltpu.CompilerParams(collective_id=0, has_side_effects=True),
        name="collect",
    )(*weights, *slabs)
    full = [w.reshape((-1,) + w.shape[2:]) for w in got[:count]]
    row = lax.axis_index("rows")
    wide = []
    for k, slab in enumerate(slabs):
        before, after = [], []
        for n, (at, by, _) in enumerate(plan):
            if at == k:
                zero = jnp.zeros((), BF)
                before.insert(0, jnp.where(row >= by, got[count + 2 * n], zero))
                after.append(jnp.where(row + by < size, got[count + 2 * n + 1], zero))
        wide.append(jnp.concatenate(before + [slab] + after, axis=2))
    return full, wide


def across_kernel(size, mine_ref, out_ref, send, recv, own):
    me = lax.axis_index("segment")
    twin = me + 1 - 2 * (me % 2)
    chips = size // 2
    others = [(me + 2 * k) % size for k in range(1, chips)]
    barrier = pltpu.get_barrier_semaphore()
    for other in [twin] + others:
        pl.semaphore_signal(barrier, inc=1, device_id={"segment": other}, device_id_type=MESH)
    pl.semaphore_wait(barrier, chips)

    def copy(n, source, slot, other):
        return pltpu.make_async_remote_copy(
            src_ref=source,
            dst_ref=out_ref.at[slot],
            send_sem=send.at[n],
            recv_sem=recv.at[n],
            device_id={"segment": other},
            device_id_type=MESH,
        )

    far = [copy(k, mine_ref, me, other) for k, other in enumerate(others)]
    for one in far:
        one.start()
    near = copy(chips - 1, mine_ref, me, twin)
    near.start()
    keep = pltpu.make_async_copy(mine_ref, out_ref.at[me], own.at[0])
    keep.start()
    passed = []
    for k in range(1, chips):
        far[k - 1].wait_recv()
        origin = (me + size - 2 * k) % size
        on = copy(chips - 1 + k, out_ref.at[origin], origin, twin)
        on.start()
        passed.append(on)
    for one in far:
        one.wait_send()
    near.wait()
    for on in passed:
        on.wait()
    keep.wait()


def across(mine, number):
    size = lax.axis_size("segment")
    count = 2 * (size // 2) - 1
    return pl.pallas_call(
        functools.partial(across_kernel, size),
        in_specs=[pl.BlockSpec(memory_space=pltpu.VMEM)],
        out_specs=pl.BlockSpec(memory_space=pltpu.VMEM),
        out_shape=jax.ShapeDtypeStruct((size,) + mine.shape, mine.dtype),
        scratch_shapes=[
            pltpu.SemaphoreType.DMA((count,)),
            pltpu.SemaphoreType.DMA((count,)),
            pltpu.SemaphoreType.DMA((1,)),
        ],
        compiler_params=pltpu.CompilerParams(collective_id=number, has_side_effects=True),
        name="across",
    )(mine)


def stack_columns(window):
    columns = window.shape[3]
    wide = jnp.pad(window, ((0, 0), (0, 0), (0, 0), (1, 1), (0, 0)))
    return jnp.concatenate(
        [wide[:, :, :, j : j + columns] for j in range(3)], axis=-1
    )


def convolve(window, weight, out_width):
    videos, frames, rows, columns, channels = window.shape
    stacked = stack_columns(window).reshape(-1, 3 * channels)
    product = jnp.dot(stacked, weight, preferred_element_type=F32)
    product = product.reshape(videos, frames, rows, columns, 9 * out_width)
    total = None
    for t in range(3):
        for i in range(3):
            tap = 3 * t + i
            term = product[
                :, t : t + frames - 2, i : i + rows - 2, :, tap * out_width : (tap + 1) * out_width
            ]
            total = term if total is None else total + term
    return total


def selector(rows, columns, offset, fine, transposed=False):
    shape = (columns, rows) if transposed else (rows, columns)
    source = lax.broadcasted_iota(jnp.int32, shape, 1 if transposed else 0) + offset
    at = lax.broadcasted_iota(jnp.int32, shape, 0 if transposed else 1)
    hit = (source == at) if fine else ((source == 2 * at) | (source == 2 * at + 1))
    return jnp.where(hit, 1.0, 0.0).astype(BF)


def picked(a, b):
    return jnp.dot(a, b, preferred_element_type=F32).astype(BF)


def middle_kernel(cache_ref, low_ref, straight_ref, weight_ref, proj_ref, keep_ref, out_ref, stacked, product, plain):
    _, past, rows, columns, channels = cache_ref.shape
    frames = low_ref.shape[1]
    width = proj_ref.shape[1]
    half = columns // 2
    line = rows * columns
    inner = rows - 2
    fine = jnp.concatenate([selector(columns, columns, j - 1, True) for j in range(3)], axis=0)
    coarse = jnp.concatenate([selector(columns, half, j - 1, False) for j in range(3)], axis=0)

    def put(at, row):
        for j in range(3):
            stacked[pl.ds(at, columns), j * channels : (j + 1) * channels] = row[
                j * columns : (j + 1) * columns
            ]

    def old(w, _):
        for q in range(rows):
            put(pl.multiple_of(w * line + q * columns, columns), picked(fine, cache_ref[0, w, q]))
        return 0

    def new(f, _):
        for l in range(rows // 2):
            row = picked(coarse, low_ref[0, f, l])
            at = pl.multiple_of((f + past) * line + 2 * l * columns, columns)
            put(at, row)
            put(at + columns, row)
        return 0

    lax.fori_loop(0, past, old, 0)
    lax.fori_loop(0, frames, new, 0)

    coarse = selector(columns, half, 0, False)

    def multiply(w, _):
        at = pl.multiple_of(w * line, line)
        product[w] = jnp.dot(
            stacked[pl.ds(at, line), :], weight_ref[...], preferred_element_type=F32
        )
        return 0

    lax.fori_loop(0, frames + past, multiply, 0)

    for f in range(frames):
        for q in range(inner):
            plain[q * columns : (q + 1) * columns, :] = picked(
                coarse, straight_ref[0, f, (q + 1) // 2]
            )
        total = jnp.dot(plain[...], proj_ref[...], preferred_element_type=F32)
        for t in range(3):
            for i in range(3):
                tap = 3 * t + i
                total = total + product[
                    f + t,
                    i * columns : (i + inner) * columns,
                    tap * width : (tap + 1) * width,
                ]
        total = jnp.where(keep_ref[...] > 0.0, total, 0.0)
        out_ref[0, :, f * inner * columns : (f + 1) * inner * columns] = total.T.astype(BF)


def middle(cache, low, straight, weight, proj, keep):
    videos, past, rows, columns, channels = cache.shape
    frames = low.shape[1]
    width = proj.shape[1]
    cells = (rows - 2) * columns

    def one(shape):
        return pl.BlockSpec((1,) + shape[1:], lambda v: (v,) + (0,) * (len(shape) - 1))

    def whole(shape):
        return pl.BlockSpec(shape, lambda v: (0,) * len(shape))

    return pl.pallas_call(
        middle_kernel,
        grid=(videos,),
        in_specs=[
            one(cache.shape),
            one(low.shape),
            one(straight.shape),
            whole(weight.shape),
            whole(proj.shape),
            whole(keep.shape),
        ],
        out_specs=one((videos, width, frames * cells)),
        out_shape=jax.ShapeDtypeStruct((videos, width, frames * cells), BF),
        scratch_shapes=[
            pltpu.VMEM(((frames + past) * rows * columns, 3 * channels), BF),
            pltpu.VMEM((frames + past, rows * columns, weight.shape[1]), F32),
            pltpu.VMEM((cells, channels), BF),
        ],
        compiler_params=pltpu.CompilerParams(vmem_limit_bytes=56 * 1024 * 1024),
        name="middle",
    )(cache, low, straight, weight, proj, keep)


def last_kernel(old_ref, cache_ref, low_ref, straight_ref, weight_ref, proj_ref, out_ref, stacked, plain, held):
    videos, taken, rows, channels, columns = cache_ref.shape
    half = columns // 2
    inner = rows - 2

    def spread(offset):
        pair = (2 * half, 2 * columns)
        source = lax.broadcasted_iota(jnp.int32, pair, 1)
        second = source >= columns
        source = jnp.where(second, source - columns, source) + offset
        at = lax.broadcasted_iota(jnp.int32, pair, 0)
        lower = at >= half
        at = jnp.where(lower, at - half, at)
        hit = ((source == 2 * at) | (source == 2 * at + 1)) & (second == lower)
        return jnp.where(hit, 1.0, 0.0).astype(BF)

    def put(t, j, q, value):
        stacked[t, j * channels : (j + 1) * channels, q * columns : (q + 1) * columns] = value

    for t in range(3):
        flag = old_ref[t]

        @pl.when(flag > 0)
        def _():
            for j in range(3):
                fine = selector(columns, columns, j - 1, True, transposed=True)
                for q in range(rows):
                    put(t, j, q, picked(cache_ref[0, t, q], fine))

        @pl.when(flag == 0)
        def _():
            for j in range(3):
                coarse = spread(j - 1)
                for p in range((rows + 2) // 4):
                    at = (t * (rows // 2 + 1) + 2 * p) * half
                    both = picked(low_ref[0, :, at : at + 2 * half], coarse)
                    for part in range(2):
                        for q in (4 * p + 2 * part - 1, 4 * p + 2 * part):
                            if 0 <= q < rows:
                                put(t, j, q, both[:, part * columns : (part + 1) * columns])

    coarse = spread(0)
    for p in range((rows + 2) // 4):
        at = 2 * p * half
        both = picked(straight_ref[0, :, at : at + 2 * half], coarse)
        for part in range(2):
            for q in (4 * p + 2 * part - 1, 4 * p + 2 * part):
                if 1 <= q <= inner:
                    plain[:, (q - 1) * columns : q * columns] = both[
                        :, part * columns : (part + 1) * columns
                    ]

    total = jnp.dot(proj_ref[...], plain[...], preferred_element_type=F32)
    for t in range(3):
        for i in range(3):
            total = total + jnp.dot(
                weight_ref[3 * t + i],
                stacked[t, :, i * columns : (i + inner) * columns],
                preferred_element_type=F32,
            )
    for q in range(inner):
        held[:, q, :] = total[:, q * columns : (q + 1) * columns]
    out_ref[0, 0] = held[...].astype(BF)


def last(old, cache, low, straight, weight, proj):
    videos, taken, rows, channels, columns = cache.shape
    width = proj.shape[0]

    def one(shape):
        return pl.BlockSpec((1,) + shape[1:], lambda v, old: (v,) + (0,) * (len(shape) - 1))

    def whole(shape):
        return pl.BlockSpec(shape, lambda v, old: (0,) * len(shape))

    out = (videos, 1, width, rows - 2, columns)
    return pl.pallas_call(
        last_kernel,
        grid_spec=pltpu.PrefetchScalarGridSpec(
            num_scalar_prefetch=1,
            grid=(videos,),
            in_specs=[
                one(cache.shape),
                one(low.shape),
                one(straight.shape),
                whole(weight.shape),
                whole(proj.shape),
            ],
            out_specs=one(out),
            scratch_shapes=[
                pltpu.VMEM((3, 3 * channels, rows * columns), BF),
                pltpu.VMEM((channels, (rows - 2) * columns), BF),
                pltpu.VMEM((width, rows - 2, columns), F32),
            ],
        ),
        out_shape=jax.ShapeDtypeStruct(out, BF),
        compiler_params=pltpu.CompilerParams(vmem_limit_bytes=56 * 1024 * 1024),
        name="last",
    )(old, cache, low, straight, weight, proj)


def shards(
    features,
    cache_zero,
    cache_one,
    cache_two,
    cache_three,
    gain_zero,
    gain_one,
    gain_two,
    gain_three,
    weight_zero,
    weight_one,
    weight_two,
    weight_three,
    proj_two,
    proj_three,
):
    segments = lax.axis_size("segment")
    segment = lax.axis_index("segment")
    row_devices = lax.axis_size("rows")
    row = lax.axis_index("rows")
    frames = features.shape[1]

    def own_channels(array):
        width = array.shape[-1] // segments
        return lax.dynamic_slice_in_dim(array, segment * width, width, array.ndim - 1)

    def flat(weight):
        return weight.reshape(weight.shape[0], -1)

    full, slabs = collect(
        [
            flat(own_channels(weight_zero)),
            flat(own_channels(weight_one)),
            flat(own_channels(weight_two)),
            flat(weight_three),
        ],
        [features, cache_zero, cache_one, cache_two, cache_three.transpose(0, 1, 2, 4, 3)],
        [2, 2, 2, 2, 1],
    )
    wide = slabs[0]
    caches = slabs[1:]

    def channels_joined(blocks):
        return jnp.concatenate([blocks[k] for k in range(segments)], axis=-1)

    def inside(array, halo):
        rows = array.shape[2]
        at = lax.broadcasted_iota(jnp.int32, (1, 1, rows, 1, 1), 2)
        keep = ((at >= halo) | (row > 0)) & ((at < rows - halo) | (row < row_devices - 1))
        return jnp.where(keep, array, jnp.zeros((), array.dtype))

    width = weight_zero.shape[3] // segments
    window = jnp.concatenate([caches[0], activate(wide, gain_zero)], axis=1)
    total = convolve(window, full[0], width)
    total = total + own_channels(wide[:, :, 1:-1]).astype(F32)
    mine = inside(total.astype(BF), 1)
    coarse = channels_joined(across(mine, 1))

    width = weight_one.shape[3] // segments
    window = jnp.concatenate([caches[1], enlarge(activate(coarse, gain_one), 2)], axis=1)
    total = convolve(window, full[1], width)
    total = total + enlarge(mine, 2)[:, :, 1:-1].astype(F32)
    mine = inside(total.astype(BF), 1)
    coarse = channels_joined(across(mine, 2))

    width = weight_two.shape[3] // segments
    rows = caches[2].shape[2] - 2
    columns = caches[2].shape[3]
    at = lax.broadcasted_iota(jnp.int32, (rows * columns, 1), 0) // columns
    keep = ((at >= 1) | (row > 0)) & ((at < rows - 1) | (row < row_devices - 1))
    mine = middle(
        caches[2],
        activate(coarse, gain_two),
        coarse,
        full[2],
        own_channels(proj_two),
        keep.astype(F32),
    )
    coarse = jnp.concatenate([blocks for blocks in across(mine, 3)], axis=1)

    own = frames // segments
    videos, channels = coarse.shape[:2]
    cells = rows * columns
    ahead = jnp.zeros((videos, channels, 2 * cells), BF)
    recent = lax.dynamic_slice_in_dim(
        jnp.concatenate([ahead, coarse], axis=2), segment * own * cells, (own + 2) * cells, 2
    )
    widened = recent.astype(F32)
    widened = widened * lax.rsqrt(
        jnp.mean(widened * widened, axis=1, keepdims=True) + EPSILON
    )
    newest = jax.nn.silu(widened * gain_three[:, None]).astype(BF)
    behind = caches[3]
    behind = jnp.pad(behind, ((0, 0), (0, own), (0, 0), (0, 0), (0, 0)))
    swapped = jnp.concatenate([behind[:, 1:2], behind[:, 2:3], behind[:, 2:3]], axis=1)
    behind = jnp.where(segment * own == 0, behind, swapped)
    old = (segment * own + jnp.arange(own + 2, dtype=jnp.int32) < 2).astype(jnp.int32)
    taps = full[3].reshape(full[3].shape[0], 9, -1).transpose(1, 2, 0)
    return last(old, behind, newest, recent[:, :, 2 * cells :], taps, proj_three.T)


def solution(mesh):
    slab = P(None, None, "rows", None, None)
    weight = P("rows", None, None, None)
    placed = (slab,) * 5 + (P(),) * 4 + (weight,) * 4 + (P(),) * 2
    return jax.shard_map(
        shards,
        mesh=mesh,
        in_specs=placed,
        out_specs=P(None, "segment", None, "rows", None),
        check_vma=False,
    )
```

```python
import functools

import jax
import jax.numpy as jnp
from jax import lax
from jax.experimental import pallas as pl
from jax.experimental.pallas import tpu as pltpu
from jax.sharding import PartitionSpec as P

EPSILON = 1e-06
BF = jnp.bfloat16
F32 = jnp.float32


def activate(values, gain_vec):
    widened = values.astype(F32)
    scaled = widened * lax.rsqrt(jnp.mean(widened * widened, axis=-1, keepdims=True) + EPSILON)
    return jax.nn.silu(scaled * gain_vec).astype(BF)


def enlarge(values, dim):
    return jnp.repeat(jnp.repeat(values, 2, axis=dim), 2, axis=dim + 1)


MESH = pl.DeviceIdType.MESH


def ring_place(row, size):
    return jnp.where(row % 2 == 0, row // 2, size - 1 - row // 2)


def ring_row(place, size):
    return jnp.where(place < size // 2, 2 * place, 2 * (size - 1 - place) + 1)


def halo_plan(shapes, widths):
    plan = []
    for k, (shape, width) in enumerate(zip(shapes, widths)):
        by = 1
        while width > 0:
            take = min(width, shape[2])
            plan.append((k, by, take))
            width -= take
            by += 1
    return plan


def collect_kernel(size, weights, slabs, plan, *refs):
    shards = refs[:weights]
    edges = refs[weights : weights + slabs]
    refs = refs[weights + slabs :]
    whole = refs[:weights]
    halos = refs[weights : weights + 2 * len(plan)]
    send, recv, own, edge_send, edge_recv, pass_send, pass_recv = refs[weights + 2 * len(plan) :]
    row = lax.axis_index("rows")
    core = lax.axis_index("segment") % 2
    twin = lax.axis_index("segment") + 1 - 2 * core
    place = ring_place(row, size)
    ahead = ring_row((place + 1) % size, size)
    back = ring_row((place + size - 1) % size, size)
    far = max(by for _, by, _ in plan)

    barrier = pltpu.get_barrier_semaphore()
    pl.semaphore_signal(barrier, inc=1, device_id={"rows": ahead}, device_id_type=MESH)
    pl.semaphore_signal(barrier, inc=1, device_id={"rows": back}, device_id_type=MESH)
    pl.semaphore_signal(barrier, inc=1, device_id={"segment": twin}, device_id_type=MESH)
    for by in range(1, far + 1):

        @pl.when(row + by < size)
        def _():
            pl.semaphore_signal(barrier, inc=1, device_id={"rows": row + by}, device_id_type=MESH)

        @pl.when(row >= by)
        def _():
            pl.semaphore_signal(barrier, inc=1, device_id={"rows": row - by}, device_id_type=MESH)

    peers = 3 + jnp.minimum(row, far) + jnp.minimum(size - 1 - row, far)
    pl.semaphore_wait(barrier, peers)

    def hop(k, way, step):
        origin = (place + size - step) % size if way == 0 else (place + step) % size
        origin = ring_row(origin, size)
        return pltpu.make_async_remote_copy(
            src_ref=shards[k] if step == 0 else whole[k].at[origin],
            dst_ref=whole[k].at[origin],
            send_sem=send.at[k, way, step],
            recv_sem=recv.at[k, way, step],
            device_id={"rows": ahead if way == 0 else back},
            device_id_type=MESH,
        )

    def edge(n, way):
        k, by, take = plan[n]
        rows = edges[k].shape[2]
        first = rows - take if way == 0 else 0
        other = row + by if way == 0 else row - by
        return pltpu.make_async_remote_copy(
            src_ref=edges[k].at[:, :, first : first + take],
            dst_ref=halos[2 * n + way],
            send_sem=edge_send.at[n, way],
            recv_sem=edge_recv.at[n, way],
            device_id={"rows": jnp.clip(other, 0, size - 1)},
            device_id_type=MESH,
        )

    def pass_on(n, way):
        return pltpu.make_async_remote_copy(
            src_ref=halos[2 * n + way],
            dst_ref=halos[2 * n + way],
            send_sem=pass_send.at[n, way],
            recv_sem=pass_recv.at[n, way],
            device_id={"segment": twin},
            device_id_type=MESH,
        )

    def steps(k, way):
        return size // 2 - (way != min(k % 3, 1))

    def each_edge(action):
        for n, (_, by, _) in enumerate(plan):
            above, below = row >= by, row + by < size
            action(n, 0, below, above, core == n % 2)
            action(n, 1, above, below, core == (n + 1) % 2)

    def start(n, way, sends, receives, mine):
        @pl.when(sends & mine)
        def _():
            edge(n, way).start()

    def relay(n, way, sends, receives, mine):
        @pl.when(receives & mine)
        def _():
            edge(n, way).wait_recv()
            pass_on(n, way).start()

    def finish(n, way, sends, receives, mine):
        @pl.when(sends & mine)
        def _():
            edge(n, way).wait_send()

        @pl.when(receives & mine)
        def _():
            pass_on(n, way).wait_send()

        @pl.when(receives & jnp.logical_not(mine))
        def _():
            pass_on(n, way).wait_recv()

    local = []
    for k in range(weights):
        for way in range(2):
            if steps(k, way) > 0:
                hop(k, way, 0).start()
        copy = pltpu.make_async_copy(shards[k], whole[k].at[row], own.at[k])
        copy.start()
        local.append(copy)
    each_edge(start)
    for step in range(size // 2):
        for k in range(weights):
            for way in range(2):
                if step < steps(k, way):
                    hop(k, way, step).wait_recv()
                    if step + 1 < steps(k, way):
                        hop(k, way, step + 1).start()
        if step == size // 2 - 2:
            each_edge(relay)
    if size // 2 < 2:
        each_edge(relay)
    for k in range(weights):
        local[k].wait()
        for way in range(2):
            for step in range(steps(k, way)):
                hop(k, way, step).wait_send()
    each_edge(finish)


def collect(weights, slabs, widths):
    size = lax.axis_size("rows")
    plan = halo_plan([slab.shape for slab in slabs], widths)
    out = [jax.ShapeDtypeStruct((size,) + w.shape, w.dtype) for w in weights]
    for k, _, take in plan:
        shape = slabs[k].shape
        out += [jax.ShapeDtypeStruct(shape[:2] + (take,) + shape[3:], BF)] * 2
    count = len(weights)
    anywhere = pl.BlockSpec(memory_space=pl.ANY)
    got = pl.pallas_call(
        functools.partial(collect_kernel, size, count, len(slabs), plan),
        in_specs=[anywhere] * (count + len(slabs)),
        out_specs=[anywhere] * len(out),
        out_shape=out,
        scratch_shapes=[
            pltpu.SemaphoreType.DMA((count, 2, size // 2 + 1)),
            pltpu.SemaphoreType.DMA((count, 2, size // 2 + 1)),
            pltpu.SemaphoreType.DMA((count,)),
            pltpu.SemaphoreType.DMA((len(plan), 2)),
            pltpu.SemaphoreType.DMA((len(plan), 2)),
            pltpu.SemaphoreType.DMA((len(plan), 2)),
            pltpu.SemaphoreType.DMA((len(plan), 2)),
        ],
        compiler_params=pltpu.CompilerParams(collective_id=0, has_side_effects=True),
        name="collect",
    )(*weights, *slabs)
    full = [w.reshape((-1,) + w.shape[2:]) for w in got[:count]]
    row = lax.axis_index("rows")
    wide = []
    for k, slab in enumerate(slabs):
        before, after = [], []
        for n, (at, by, _) in enumerate(plan):
            if at == k:
                zero = jnp.zeros((), BF)
                before.insert(0, jnp.where(row >= by, got[count + 2 * n], zero))
                after.append(jnp.where(row + by < size, got[count + 2 * n + 1], zero))
        wide.append(jnp.concatenate(before + [slab] + after, axis=2))
    return full, wide


def across_kernel(size, mine_ref, out_ref, send, recv, own):
    me = lax.axis_index("segment")
    twin = me + 1 - 2 * (me % 2)
    chips = size // 2
    others = [(me + 2 * k) % size for k in range(1, chips)]
    barrier = pltpu.get_barrier_semaphore()
    for other in [twin] + others:
        pl.semaphore_signal(barrier, inc=1, device_id={"segment": other}, device_id_type=MESH)
    pl.semaphore_wait(barrier, chips)

    def copy(n, source, slot, other):
        return pltpu.make_async_remote_copy(
            src_ref=source,
            dst_ref=out_ref.at[slot],
            send_sem=send.at[n],
            recv_sem=recv.at[n],
            device_id={"segment": other},
            device_id_type=MESH,
        )

    far = [copy(k, mine_ref, me, other) for k, other in enumerate(others)]
    for one in far:
        one.start()
    near = copy(chips - 1, mine_ref, me, twin)
    near.start()
    keep = pltpu.make_async_copy(mine_ref, out_ref.at[me], own.at[0])
    keep.start()
    passed = []
    for k in range(1, chips):
        far[k - 1].wait_recv()
        origin = (me + size - 2 * k) % size
        on = copy(chips - 1 + k, out_ref.at[origin], origin, twin)
        on.start()
        passed.append(on)
    for one in far:
        one.wait_send()
    near.wait()
    for on in passed:
        on.wait()
    keep.wait()


def across(mine, number):
    size = lax.axis_size("segment")
    count = 2 * (size // 2) - 1
    return pl.pallas_call(
        functools.partial(across_kernel, size),
        in_specs=[pl.BlockSpec(memory_space=pltpu.VMEM)],
        out_specs=pl.BlockSpec(memory_space=pltpu.VMEM),
        out_shape=jax.ShapeDtypeStruct((size,) + mine.shape, mine.dtype),
        scratch_shapes=[
            pltpu.SemaphoreType.DMA((count,)),
            pltpu.SemaphoreType.DMA((count,)),
            pltpu.SemaphoreType.DMA((1,)),
        ],
        compiler_params=pltpu.CompilerParams(collective_id=number, has_side_effects=True),
        name="across",
    )(mine)


def stack_columns(window):
    columns = window.shape[3]
    wide = jnp.pad(window, ((0, 0), (0, 0), (0, 0), (1, 1), (0, 0)))
    return jnp.concatenate(
        [wide[:, :, :, j : j + columns] for j in range(3)], axis=-1
    )


def convolve(window, weight, out_width):
    videos, frames, rows, columns, channels = window.shape
    stacked = stack_columns(window).reshape(-1, 3 * channels)
    product = jnp.dot(stacked, weight, preferred_element_type=F32)
    product = product.reshape(videos, frames, rows, columns, 9 * out_width)
    total = None
    for t in range(3):
        for i in range(3):
            tap = 3 * t + i
            term = product[
                :, t : t + frames - 2, i : i + rows - 2, :, tap * out_width : (tap + 1) * out_width
            ]
            total = term if total is None else total + term
    return total


def selector(rows, columns, offset, fine, transposed=False):
    shape = (columns, rows) if transposed else (rows, columns)
    source = lax.broadcasted_iota(jnp.int32, shape, 1 if transposed else 0) + offset
    at = lax.broadcasted_iota(jnp.int32, shape, 0 if transposed else 1)
    hit = (source == at) if fine else ((source == 2 * at) | (source == 2 * at + 1))
    return jnp.where(hit, 1.0, 0.0).astype(BF)


def picked(a, b):
    return jnp.dot(a, b, preferred_element_type=F32).astype(BF)


def middle_kernel(cache_ref, low_ref, straight_ref, weight_ref, proj_ref, keep_ref, out_ref, stacked, product, plain):
    _, past, rows, columns, channels = cache_ref.shape
    frames = low_ref.shape[1]
    width = proj_ref.shape[1]
    half = columns // 2
    line = rows * columns
    inner = rows - 2
    fine = jnp.concatenate([selector(columns, columns, j - 1, True) for j in range(3)], axis=0)
    coarse = jnp.concatenate([selector(columns, half, j - 1, False) for j in range(3)], axis=0)

    def put(at, row):
        for j in range(3):
            stacked[pl.ds(at, columns), j * channels : (j + 1) * channels] = row[
                j * columns : (j + 1) * columns
            ]

    def old(w, _):
        for q in range(rows):
            put(pl.multiple_of(w * line + q * columns, columns), picked(fine, cache_ref[0, w, q]))
        return 0

    def new(f, _):
        for l in range(rows // 2):
            row = picked(coarse, low_ref[0, f, l])
            at = pl.multiple_of((f + past) * line + 2 * l * columns, columns)
            put(at, row)
            put(at + columns, row)
        return 0

    lax.fori_loop(0, past, old, 0)
    lax.fori_loop(0, frames, new, 0)

    coarse = selector(columns, half, 0, False)

    def multiply(w, _):
        at = pl.multiple_of(w * line, line)
        product[w] = jnp.dot(
            stacked[pl.ds(at, line), :], weight_ref[...], preferred_element_type=F32
        )
        return 0

    lax.fori_loop(0, frames + past, multiply, 0)

    for f in range(frames):
        for q in range(inner):
            plain[q * columns : (q + 1) * columns, :] = picked(
                coarse, straight_ref[0, f, (q + 1) // 2]
            )
        total = jnp.dot(plain[...], proj_ref[...], preferred_element_type=F32)
        for t in range(3):
            for i in range(3):
                tap = 3 * t + i
                total = total + product[
                    f + t,
                    i * columns : (i + inner) * columns,
                    tap * width : (tap + 1) * width,
                ]
        total = jnp.where(keep_ref[...] > 0.0, total, 0.0)
        out_ref[0, :, f * inner * columns : (f + 1) * inner * columns] = total.T.astype(BF)


def middle(cache, low, straight, weight, proj, keep):
    videos, past, rows, columns, channels = cache.shape
    frames = low.shape[1]
    width = proj.shape[1]
    cells = (rows - 2) * columns

    def one(shape):
        return pl.BlockSpec((1,) + shape[1:], lambda v: (v,) + (0,) * (len(shape) - 1))

    def whole(shape):
        return pl.BlockSpec(shape, lambda v: (0,) * len(shape))

    return pl.pallas_call(
        middle_kernel,
        grid=(videos,),
        in_specs=[
            one(cache.shape),
            one(low.shape),
            one(straight.shape),
            whole(weight.shape),
            whole(proj.shape),
            whole(keep.shape),
        ],
        out_specs=one((videos, width, frames * cells)),
        out_shape=jax.ShapeDtypeStruct((videos, width, frames * cells), BF),
        scratch_shapes=[
            pltpu.VMEM(((frames + past) * rows * columns, 3 * channels), BF),
            pltpu.VMEM((frames + past, rows * columns, weight.shape[1]), F32),
            pltpu.VMEM((cells, channels), BF),
        ],
        compiler_params=pltpu.CompilerParams(vmem_limit_bytes=56 * 1024 * 1024),
        name="middle",
    )(cache, low, straight, weight, proj, keep)


def last_kernel(old_ref, cache_ref, low_ref, straight_ref, weight_ref, proj_ref, out_ref, stacked, plain, held):
    videos, taken, rows, channels, columns = cache_ref.shape
    half = columns // 2
    inner = rows - 2

    def spread(offset):
        pair = (2 * half, 2 * columns)
        source = lax.broadcasted_iota(jnp.int32, pair, 1)
        second = source >= columns
        source = jnp.where(second, source - columns, source) + offset
        at = lax.broadcasted_iota(jnp.int32, pair, 0)
        lower = at >= half
        at = jnp.where(lower, at - half, at)
        hit = ((source == 2 * at) | (source == 2 * at + 1)) & (second == lower)
        return jnp.where(hit, 1.0, 0.0).astype(BF)

    def put(t, j, q, value):
        stacked[t, j * channels : (j + 1) * channels, q * columns : (q + 1) * columns] = value

    for t in range(3):
        flag = old_ref[t]

        @pl.when(flag >= 0)
        def _():
            for j in range(3):
                fine = selector(columns, columns, j - 1, True, transposed=True)
                for q in range(rows):
                    put(t, j, q, picked(cache_ref[0, jnp.maximum(flag, 0), q], fine))

        @pl.when(flag < 0)
        def _():
            for j in range(3):
                coarse = spread(j - 1)
                for p in range((rows + 2) // 4):
                    at = (t * (rows // 2 + 1) + 2 * p) * half
                    both = picked(low_ref[0, :, at : at + 2 * half], coarse)
                    for part in range(2):
                        for q in (4 * p + 2 * part - 1, 4 * p + 2 * part):
                            if 0 <= q < rows:
                                put(t, j, q, both[:, part * columns : (part + 1) * columns])

    coarse = spread(0)
    for p in range((rows + 2) // 4):
        at = 2 * p * half
        both = picked(straight_ref[0, :, at : at + 2 * half], coarse)
        for part in range(2):
            for q in (4 * p + 2 * part - 1, 4 * p + 2 * part):
                if 1 <= q <= inner:
                    plain[:, (q - 1) * columns : q * columns] = both[
                        :, part * columns : (part + 1) * columns
                    ]

    total = jnp.dot(proj_ref[...], plain[...], preferred_element_type=F32)
    for t in range(3):
        for i in range(3):
            total = total + jnp.dot(
                weight_ref[3 * t + i],
                stacked[t, :, i * columns : (i + inner) * columns],
                preferred_element_type=F32,
            )
    for q in range(inner):
        held[:, q, :] = total[:, q * columns : (q + 1) * columns]
    out_ref[0, 0] = held[...].astype(BF)


def last(old, cache, low, straight, weight, proj):
    videos, taken, rows, channels, columns = cache.shape
    width = proj.shape[0]

    def one(shape):
        return pl.BlockSpec((1,) + shape[1:], lambda v, old: (v,) + (0,) * (len(shape) - 1))

    def whole(shape):
        return pl.BlockSpec(shape, lambda v, old: (0,) * len(shape))

    out = (videos, 1, width, rows - 2, columns)
    return pl.pallas_call(
        last_kernel,
        grid_spec=pltpu.PrefetchScalarGridSpec(
            num_scalar_prefetch=1,
            grid=(videos,),
            in_specs=[
                one(cache.shape),
                one(low.shape),
                one(straight.shape),
                whole(weight.shape),
                whole(proj.shape),
            ],
            out_specs=one(out),
            scratch_shapes=[
                pltpu.VMEM((3, 3 * channels, rows * columns), BF),
                pltpu.VMEM((channels, (rows - 2) * columns), BF),
                pltpu.VMEM((width, rows - 2, columns), F32),
            ],
        ),
        out_shape=jax.ShapeDtypeStruct(out, BF),
        compiler_params=pltpu.CompilerParams(vmem_limit_bytes=56 * 1024 * 1024),
        name="last",
    )(old, cache, low, straight, weight, proj)


def shards(
    features,
    cache_zero,
    cache_one,
    cache_two,
    cache_three,
    gain_zero,
    gain_one,
    gain_two,
    gain_three,
    weight_zero,
    weight_one,
    weight_two,
    weight_three,
    proj_two,
    proj_three,
):
    segments = lax.axis_size("segment")
    segment = lax.axis_index("segment")
    row_devices = lax.axis_size("rows")
    row = lax.axis_index("rows")
    frames = features.shape[1]

    def own_channels(array):
        width = array.shape[-1] // segments
        return lax.dynamic_slice_in_dim(array, segment * width, width, array.ndim - 1)

    def flat(weight):
        return weight.reshape(weight.shape[0], -1)

    full, slabs = collect(
        [
            flat(own_channels(weight_zero)),
            flat(own_channels(weight_one)),
            flat(own_channels(weight_two)),
            flat(weight_three),
        ],
        [features, cache_zero, cache_one, cache_two, cache_three.transpose(0, 1, 2, 4, 3)],
        [2, 2, 2, 2, 1],
    )
    wide = slabs[0]
    caches = slabs[1:]

    def channels_joined(blocks):
        return jnp.concatenate([blocks[k] for k in range(segments)], axis=-1)

    def inside(array, halo):
        rows = array.shape[2]
        at = lax.broadcasted_iota(jnp.int32, (1, 1, rows, 1, 1), 2)
        keep = ((at >= halo) | (row > 0)) & ((at < rows - halo) | (row < row_devices - 1))
        return jnp.where(keep, array, jnp.zeros((), array.dtype))

    width = weight_zero.shape[3] // segments
    window = jnp.concatenate([caches[0], activate(wide, gain_zero)], axis=1)
    total = convolve(window, full[0], width)
    total = total + own_channels(wide[:, :, 1:-1]).astype(F32)
    mine = inside(total.astype(BF), 1)
    coarse = channels_joined(across(mine, 1))

    width = weight_one.shape[3] // segments
    window = jnp.concatenate([caches[1], enlarge(activate(coarse, gain_one), 2)], axis=1)
    total = convolve(window, full[1], width)
    total = total + enlarge(mine, 2)[:, :, 1:-1].astype(F32)
    mine = inside(total.astype(BF), 1)
    coarse = channels_joined(across(mine, 2))

    width = weight_two.shape[3] // segments
    rows = caches[2].shape[2] - 2
    columns = caches[2].shape[3]
    at = lax.broadcasted_iota(jnp.int32, (rows * columns, 1), 0) // columns
    keep = ((at >= 1) | (row > 0)) & ((at < rows - 1) | (row < row_devices - 1))
    mine = middle(
        caches[2],
        activate(coarse, gain_two),
        coarse,
        full[2],
        own_channels(proj_two),
        keep.astype(F32),
    )
    coarse = jnp.concatenate([blocks for blocks in across(mine, 3)], axis=1)

    own = frames // segments
    videos, channels = coarse.shape[:2]
    cells = rows * columns
    ahead = jnp.zeros((videos, channels, 2 * cells), BF)
    recent = lax.dynamic_slice_in_dim(
        jnp.concatenate([ahead, coarse], axis=2), segment * own * cells, (own + 2) * cells, 2
    )
    widened = recent.astype(F32)
    widened = widened * lax.rsqrt(
        jnp.mean(widened * widened, axis=1, keepdims=True) + EPSILON
    )
    newest = jax.nn.silu(widened * gain_three[:, None]).astype(BF)
    at = segment * own + jnp.arange(own + 2, dtype=jnp.int32)
    old = jnp.where(at < 2, at, -1)
    taps = full[3].reshape(full[3].shape[0], 9, -1).transpose(1, 2, 0)
    return last(old, caches[3], newest, recent[:, :, 2 * cells :], taps, proj_three.T)


def solution(mesh):
    slab = P(None, None, "rows", None, None)
    weight = P("rows", None, None, None)
    placed = (slab,) * 5 + (P(),) * 4 + (weight,) * 4 + (P(),) * 2
    return jax.shard_map(
        shards,
        mesh=mesh,
        in_specs=placed,
        out_specs=P(None, "segment", None, "rows", None),
        check_vma=False,
    )
```
